32 devices in a mesh: island: 8 (over z, x), fsdp: 4 (over y, core).
Axes of the slice: x: 2, y: 2, z: 4, core: 2. Of those that a mesh axis runs over, the one named last changes fastest.
Arguments:
- local_weights: bfloat16 [8, 4096, 512], P('island', 'fsdp'), may hold values from -6 to 6
- adam_first: bfloat16 [8, 4096, 512], P('island', 'fsdp'), may hold values from -6 to 6
- adam_second: bfloat16 [8, 4096, 512], P('island', 'fsdp'), may hold values from 0.5 to 4
- global_weights: float32 [4096, 512], P('fsdp'), may hold values from -6 to 6
- outer_momentum: float32 [4096, 512], P('fsdp'), may hold values from -3 to 3
- inputs: bfloat16 [8, 512, 4096], P('island', 'fsdp'), may hold values from -6 to 6
- key_cotangent: bfloat16 [8, 512, 512], P('island', 'fsdp'), may hold values from -24 to 24
Outputs:
- new_local: bfloat16 [8, 4096, 512], P('island', 'fsdp')
- new_first: bfloat16 [8, 4096, 512], P('island', 'fsdp')
- new_second: bfloat16 [8, 4096, 512], P('island', 'fsdp')
- new_global: float32 [4096, 512], P('fsdp')
- new_momentum: float32 [4096, 512], P('fsdp')
The draws below stay inside these ranges and needn't reach their ends.
All inputs are finite; a program needn't handle non-finite values.
Results may differ from the reference program's by a relative error of at most 0.0065.
Values may be sent and summed in bfloat16 or wider, within the bound.
A program may use at most 64 MiB of HBM per device.

```python
import math
import jax
import jax.numpy as jnp
from jax import lax

D = 4096
KV_HEADS = 4
HEAD_DIM = 128
TOK_DEV = 128
KEY_WIDTH = 512
ISLAND_TOKENS = 512
N_ISLAND = 8
N_FSDP = 4


def level_of(rng, shape, cuts, smallest, top_value):
    gain = 1.0
    for dim, blocks in cuts:
        draws = jax.random.uniform(jax.random.fold_in(jax.random.fold_in(rng, 6), dim), (blocks,), jnp.float32, smallest / len(cuts), top_value / len(cuts))
        gain = gain * jnp.repeat(jnp.exp(draws), shape[dim] // blocks).reshape((-1,) + (1,) * (len(shape) - 1 - dim))
    return gain


def centred(own_key, extent, width, most, split=(), dtype=jnp.bfloat16):
    result = width * jax.random.normal(own_key, extent, jnp.float32)
    if split:
        result = result * level_of(own_key, extent, split, -0.22, 0.18)
    return jnp.clip(result, -most, most).astype(dtype)


def setup_inputs(seed: int = 0) -> dict:
    key_list = jax.random.split(jax.random.key(seed), 8)
    local_weights = centred(key_list[0], (N_ISLAND, D, KEY_WIDTH), 1.0, 6.0, ((0, 8), (1, 4)))
    adam_first = centred(key_list[1], (N_ISLAND, D, KEY_WIDTH), 1.0, 6.0, ((0, 8), (1, 4)))
    adam_second = jnp.clip(jnp.exp(math.log(4.0) - 2.0794415 * jax.random.uniform(key_list[2], (N_ISLAND, D, KEY_WIDTH), jnp.float32) ** level_of(key_list[2], (N_ISLAND, D, KEY_WIDTH), ((0, 8), (1, 4)), -0.2, 0.2)), 0.5, 4.0).astype(jnp.bfloat16)
    global_weights = centred(key_list[3], (D, KEY_WIDTH), 1.0, 6.0, ((0, 4),), jnp.float32)
    outer_momentum = centred(key_list[4], (D, KEY_WIDTH), 0.5, 3.0, ((0, 4),), jnp.float32)
    inputs = centred(key_list[5], (N_ISLAND, ISLAND_TOKENS, D), 1.0, 6.0, ((0, 8), (1, 4)))
    key_cotangent = centred(key_list[6], (N_ISLAND, ISLAND_TOKENS, KEY_WIDTH), 4.0, 24.0, ((0, 8), (1, 4)))
    return dict(local_weights=local_weights, adam_first=adam_first, adam_second=adam_second, global_weights=global_weights, outer_momentum=outer_momentum, inputs=inputs, key_cotangent=key_cotangent)


beta_one = 0.9
beta_two = 0.95
inner_rate = 0.02
weight_decay = 0.1
adam_epsilon = 1e-08
norm_epsilon = 1e-06
outer_rate = 0.7
outer_beta = 0.9
merge_weight = 0.5

def key_backward(keys, upstream):
    shaped = keys.reshape(keys.shape[0], KV_HEADS, HEAD_DIM)
    cotan_heads = upstream.reshape(keys.shape[0], KV_HEADS, HEAD_DIM)
    squares = lax.optimization_barrier(jnp.mean(shaped * shaped, axis=-1, keepdims=True))
    inverse = lax.rsqrt(squares + norm_epsilon)
    normed = shaped * inverse
    projected = lax.optimization_barrier(jnp.mean(cotan_heads * normed, axis=-1, keepdims=True))
    return (inverse * (cotan_heads - normed * projected)).reshape(keys.shape)

def reference(local_weights, adam_first, adam_second, global_weights, outer_momentum, inputs, key_cotangent):
    summed = lax.optimization_barrier(jnp.sum(local_weights.astype(jnp.float32), axis=0))
    outer_grad = global_weights - summed / N_ISLAND
    new_momentum = outer_beta * outer_momentum + outer_grad
    new_global = global_weights - outer_rate * (outer_grad + outer_beta * new_momentum)
    scale = float(D) ** (-0.5)

    def island_update(packed):
        weights, first_moment, second_moment, tokens, upstream = packed
        keys = jnp.dot(tokens, weights, preferred_element_type=jnp.float32) * scale
        key_grad = (key_backward(keys, upstream.astype(jnp.float32)) * scale).astype(jnp.bfloat16)
        blocks = jnp.einsum('ntd,ntk->ndk', tokens.reshape(N_FSDP, TOK_DEV, D).astype(jnp.float32), key_grad.reshape(N_FSDP, TOK_DEV, KEY_WIDTH).astype(jnp.float32))
        rounded = lax.optimization_barrier(blocks.astype(jnp.bfloat16))
        gradient = lax.optimization_barrier(jnp.sum(rounded.astype(jnp.float32), axis=0))
        first_new = beta_one * first_moment.astype(jnp.float32) + (1.0 - beta_one) * gradient
        second_new = beta_two * second_moment.astype(jnp.float32) + (1.0 - beta_two) * gradient * gradient
        current = weights.astype(jnp.float32)
        inner = current - inner_rate * (first_new / (jnp.sqrt(second_new) + adam_epsilon) + weight_decay * current)
        merged = merge_weight * inner + (1.0 - merge_weight) * new_global
        return (merged.astype(jnp.bfloat16), first_new.astype(jnp.bfloat16), second_new.astype(jnp.bfloat16))
    new_local, new_first, new_second = lax.map(island_update, (local_weights, adam_first, adam_second, inputs, key_cotangent))
    return (new_local, new_first, new_second, new_global, new_momentum)
```

```python
import functools

import jax
import jax.numpy as jnp
from jax import lax
from jax.experimental import pallas as pl
from jax.experimental.pallas import tpu as pltpu
from jax.sharding import PartitionSpec as P

HEAD_DIM = 128
MESH = pl.DeviceIdType.MESH

beta_one = 0.9
beta_two = 0.95
inner_rate = 0.02
weight_decay = 0.1
adam_epsilon = 1e-08
norm_epsilon = 1e-06
outer_rate = 0.7
outer_beta = 0.9
merge_weight = 0.5


def chunk_count(rows, islands):
    for chunks in (4, 2, 1):
        if islands % 2 == 0 and rows % (islands * chunks * 16) == 0:
            return chunks
    return 0


def head_backward(keys, upstream, scale):
    squares = jnp.mean(keys * keys, axis=-1, keepdims=True)
    inverse = lax.rsqrt(squares + norm_epsilon)
    normed = keys * inverse
    projected = jnp.mean(upstream * normed, axis=-1, keepdims=True)
    return (inverse * (upstream - normed * projected) * scale).astype(jnp.bfloat16)


def exchange(islands, shards, chunks, scale, *refs):
    w, x, cot = refs[:3]
    if chunks:
        (grad, mean, wp, xin, xp, psend, precv, kgin, kgp, kg, own,
         ysem, psem, ksem, csem, fsem, p1buf, part, p2buf, gathered,
         s1, s2, s3, s4) = refs[3:]
    else:
        (grad, wp, xin, xp, psend, precv, kgin, kgp, kg, own,
         ysem, psem, ksem, csem, fsem) = refs[3:]
    rows, width = w.shape
    chips = shards // 2
    island = lax.axis_index("island")
    shard = lax.axis_index("fsdp")
    core = lax.rem(shard, 2)
    chip = shard // 2
    partner = (island, chip * 2 + 1 - core)

    def peer(step):
        return (island, lax.rem(chip + step, chips) * 2 + core)

    def back(step):
        return (island, lax.rem(chip + chips - step, chips) * 2 + core)

    targets = [partner] + [peer(step) for step in range(1, chips)]
    if chunks:
        groups = islands // 2
        side = lax.rem(island, 2)
        line = island // 2
        across = (line * 2 + 1 - side, shard)

        def along(step):
            return (lax.rem(line + step, groups) * 2 + side, shard)

        targets += [across] + [along(step) for step in range(1, groups)]

    barrier = pltpu.get_barrier_semaphore()
    for target in targets:
        pl.semaphore_signal(barrier, inc=1, device_id=target, device_id_type=MESH)
    pl.semaphore_wait(barrier, len(targets))

    def remote(src, dst, sems, where, target):
        return pltpu.make_async_remote_copy(
            src_ref=src,
            dst_ref=dst,
            send_sem=sems.at[(0,) + where],
            recv_sem=sems.at[(1,) + where],
            device_id=target,
            device_id_type=MESH,
        )

    def columns(start):
        return pl.ds(pl.multiple_of(start, rows), rows)

    copies = []

    def begin(copy):
        copy.start()
        copies.append(copy)
        return copy

    y1 = []
    for step in range(1, chips):
        there = lax.rem(chip + step, chips)
        y1.append(begin(remote(
            x.at[:, pl.ds(pl.multiple_of(there * 2 * rows, 2 * rows), 2 * rows)],
            xin.at[step - 1], ysem, (step - 1,), peer(step))))
    if chunks:
        half = rows // 2
        size = half // chunks
        unit = size // groups
        p1 = [
            begin(remote(
                w.at[pl.ds(pl.multiple_of((1 - side) * half + q * size, size), size)],
                p1buf.at[q], s1, (q,), across))
            for q in range(chunks)
        ]
    wcopy = begin(remote(w, wp, csem, (0,), partner))
    xcopy = [begin(remote(
        x.at[:, columns((chip * 2 + 1 - core) * rows)], xp.at[0], csem, (1,), partner))]

    p2, p3, p4 = {}, {}, {}

    def pair_sum(q):
        p1[q].wait_recv()
        mine = w[pl.ds(pl.multiple_of(side * half + q * size, size), size), :]
        part[q] = (mine.astype(jnp.float32) + p1buf[q].astype(jnp.float32)).astype(jnp.bfloat16)
        for step in range(1, groups):
            there = lax.rem(line + step, groups)
            p2[q, step] = begin(remote(
                part.at[q, pl.ds(pl.multiple_of(there * unit, unit), unit)],
                p2buf.at[q, step - 1], s2, (q, step - 1), along(step)))

    def line_sum(q):
        total = part[q, pl.ds(pl.multiple_of(line * unit, unit), unit), :].astype(jnp.float32)
        for step in range(1, groups):
            p2[q, step].wait_recv()
            total += p2buf[q, step - 1].astype(jnp.float32)
        place = pl.ds(pl.multiple_of(side * half + q * size + line * unit, unit), unit)
        gathered[place, :] = (total / islands).astype(jnp.bfloat16)
        for step in range(1, groups):
            p3[q, step] = begin(remote(
                gathered.at[place], gathered.at[place], s3, (q, step - 1), along(step)))

    def return_half(q):
        for step in range(1, groups):
            p3[q, step].wait_recv()
        place = pl.ds(pl.multiple_of(side * half + q * size, size), size)
        p4[q] = begin(remote(gathered.at[place], gathered.at[place], s4, (q,), across))

    def product(left, right):
        return jnp.dot(left, right, preferred_element_type=jnp.float32)

    stages = []

    def advance(count):
        for _ in range(count):
            if stages:
                stage, q = stages.pop(0)
                stage(q)

    if chunks:
        for t in range(chunks + 4):
            if t < chunks:
                stages.append((pair_sum, t))
            if 0 <= t - 2 < chunks:
                stages.append((line_sum, t - 2))
            if 0 <= t - 4 < chunks:
                stages.append((return_half, t - 4))
    total_stages = len(stages)

    advance(2)
    wcopy.wait_recv()
    own[...] = product(x[:, columns(shard * rows)], w[...]) + product(
        x[:, columns((chip * 2 + 1 - core) * rows)], wp[...])
    advance(total_stages // 2 - 2)

    y3 = []
    for step in range(1, chips):
        y1[step - 1].wait_recv()
        xcopy.append(begin(remote(
            xin.at[step - 1, :, columns((1 - core) * rows)], xp.at[step], csem, (step + 1,), partner)))
        psend[step - 1] = product(xin[step - 1, :, columns(core * rows)], w[...]) + product(
            xin[step - 1, :, columns((1 - core) * rows)], wp[...])
        y3.append(begin(remote(
            psend.at[step - 1], precv.at[step - 1], psem, (step - 1,), back(step))))
    advance((total_stages - total_stages // 2) // 2)

    keys = own[...]
    for step in range(1, chips):
        y3[step - 1].wait_recv()
        keys += precv[step - 1]
    keys = keys * scale
    for head in range(width // HEAD_DIM):
        lanes = slice(head * HEAD_DIM, (head + 1) * HEAD_DIM)
        kg[:, lanes] = head_backward(keys[:, lanes], cot[:, lanes].astype(jnp.float32), scale)
    y4 = [
        begin(remote(kg, kgin.at[step - 1], ksem, (step - 1,), peer(step)))
        for step in range(1, chips)
    ]
    forwards = [begin(remote(kg, kgp.at[0], fsem, (0,), partner))]

    tile = min(256, rows)

    def add_block(read, upstream, first=False):
        @pl.loop(0, rows // tile)
        def _(t):
            start = pl.multiple_of(t * tile, tile)
            term = lax.dot_general(
                read(start), upstream[...], (((0,), (0,)), ((), ())),
                preferred_element_type=jnp.float32,
            ).astype(jnp.bfloat16).astype(jnp.float32)
            place = pl.ds(start, tile)
            grad[place, :] = term if first else grad[place, :] + term

    def lane(base):
        def at(start):
            return pl.ds(pl.multiple_of(base + start, tile), tile)
        return at

    mine = lane(shard * rows)
    add_block(lambda start: x[:, mine(start)], kg, first=True)
    forwards[0].wait_recv()
    xcopy[0].wait_recv()
    add_block(lambda start: xp[0, :, pl.ds(start, tile)], kgp.at[0])
    inner = lane(core * rows)
    for step in range(1, chips):
        y4[step - 1].wait_recv()
        forwards.append(begin(remote(
            kgin.at[step - 1], kgp.at[step], fsem, (step,), partner)))
        add_block(lambda start: xin[step - 1, :, inner(start)], kgin.at[step - 1])
    for step in range(1, chips):
        xcopy[step].wait_recv()
        forwards[step].wait_recv()
        add_block(lambda start: xp[step, :, pl.ds(start, tile)], kgp.at[step])
    advance(len(stages))
    if chunks:
        for q in range(chunks):
            p4[q].wait_recv()
        mean[...] = gathered[...]
    for copy in copies:
        copy.wait_send()


def local(
    local_weights, adam_first, adam_second, global_weights, outer_momentum, inputs, key_cotangent
):
    weights = local_weights[0]
    tokens = inputs[0]
    rows, width = weights.shape
    count, depth = tokens.shape
    scale = float(depth) ** (-0.5)
    islands, shards = lax.axis_size("island"), lax.axis_size("fsdp")
    chips = shards // 2
    others = max(chips - 1, 1)
    chunks = chunk_count(rows, islands)
    bf16, f32 = jnp.bfloat16, jnp.float32
    dma = pltpu.SemaphoreType.DMA
    out_shape = [jax.ShapeDtypeStruct((rows, width), f32)]
    scratch = [
        pltpu.VMEM((rows, width), bf16),
        pltpu.VMEM((others, count, 2 * rows), bf16),
        pltpu.VMEM((chips, count, rows), bf16),
        pltpu.VMEM((others, count, width), f32),
        pltpu.VMEM((others, count, width), f32),
        pltpu.VMEM((others, count, width), bf16),
        pltpu.VMEM((chips, count, width), bf16),
        pltpu.VMEM((count, width), bf16),
        pltpu.VMEM((count, width), f32),
        dma((2, others)),
        dma((2, others)),
        dma((2, others)),
        dma((2, chips + 1)),
        dma((2, chips)),
    ]
    if chunks:
        groups = islands // 2
        size = rows // 2 // chunks
        out_shape.append(jax.ShapeDtypeStruct((rows, width), bf16))
        scratch += [
            pltpu.VMEM((chunks, size, width), bf16),
            pltpu.VMEM((chunks, size, width), bf16),
            pltpu.VMEM((chunks, groups - 1, size // groups, width), bf16),
            pltpu.VMEM((rows, width), bf16),
            dma((2, chunks)),
            dma((2, chunks, groups - 1)),
            dma((2, chunks, groups - 1)),
            dma((2, chunks)),
        ]
    vmem = pl.BlockSpec(memory_space=pltpu.VMEM)
    results = pl.pallas_call(
        functools.partial(exchange, islands, shards, chunks, scale),
        out_shape=out_shape,
        in_specs=[vmem] * 3,
        out_specs=[vmem] * len(out_shape),
        scratch_shapes=scratch,
        compiler_params=pltpu.CompilerParams(
            collective_id=0, has_side_effects=True, vmem_limit_bytes=40 * 1024 * 1024
        ),
    )(weights, tokens, key_cotangent[0])
    gradient = results[0]
    if chunks:
        mean_local = results[1].astype(jnp.float32)
    else:
        mean_local = lax.psum(weights.astype(jnp.float32), "island") / islands
    outer_grad = global_weights - mean_local
    new_momentum = outer_beta * outer_momentum + outer_grad
    new_global = global_weights - outer_rate * (outer_grad + outer_beta * new_momentum)
    first_new = beta_one * adam_first[0].astype(jnp.float32) + (1.0 - beta_one) * gradient
    second_new = (
        beta_two * adam_second[0].astype(jnp.float32) + (1.0 - beta_two) * gradient * gradient
    )
    current = weights.astype(jnp.float32)
    inner = current - inner_rate * (
        first_new / (jnp.sqrt(second_new) + adam_epsilon) + weight_decay * current
    )
    merged = merge_weight * inner + (1.0 - merge_weight) * new_global
    return (
        merged.astype(jnp.bfloat16)[None],
        first_new.astype(jnp.bfloat16)[None],
        second_new.astype(jnp.bfloat16)[None],
        new_global,
        new_momentum,
    )


def solution(mesh):
    placed = (
        P("island", "fsdp", None),
        P("island", "fsdp", None),
        P("island", "fsdp", None),
        P("fsdp", None),
        P("fsdp", None),
        P("island", "fsdp", None),
        P("island", "fsdp", None),
    )
    return jax.shard_map(
        local,
        mesh=mesh,
        in_specs=placed,
        out_specs=(
            P("island", "fsdp", None),
            P("island", "fsdp", None),
            P("island", "fsdp", None),
            P("fsdp", None),
            P("fsdp", None),
        ),
        check_vma=False,
    )
```

```python
import functools

import jax
import jax.numpy as jnp
from jax import lax
from jax.experimental import pallas as pl
from jax.experimental.pallas import tpu as pltpu
from jax.sharding import PartitionSpec as P

HEAD_DIM = 128
MESH = pl.DeviceIdType.MESH

beta_one = 0.9
beta_two = 0.95
inner_rate = 0.02
weight_decay = 0.1
adam_epsilon = 1e-08
norm_epsilon = 1e-06
outer_rate = 0.7
outer_beta = 0.9
merge_weight = 0.5


def chunk_count(rows, islands):
    for chunks in (4, 2, 1):
        if islands % 2 == 0 and rows % (islands * chunks * 16) == 0:
            return chunks
    return 0


def head_backward(keys, upstream, scale):
    squares = jnp.mean(keys * keys, axis=-1, keepdims=True)
    inverse = lax.rsqrt(squares + norm_epsilon)
    normed = keys * inverse
    projected = jnp.mean(upstream * normed, axis=-1, keepdims=True)
    return (inverse * (upstream - normed * projected) * scale).astype(jnp.bfloat16)


def exchange(islands, shards, chunks, scale, *refs):
    w_hbm, x_hbm, cot_hbm = refs[:3]
    if chunks:
        (grad, mean, w, x, cot, lsem, wp, xin, xp, psend, precv, kgin, kgp, kg, own,
         ysem, psem, ksem, csem, fsem, p1buf, part, p2buf, gathered,
         s1, s2, s3, s4) = refs[3:]
    else:
        (grad, w, x, cot, lsem, wp, xin, xp, psend, precv, kgin, kgp, kg, own,
         ysem, psem, ksem, csem, fsem) = refs[3:]
    rows, width = w.shape
    chips = shards // 2
    island = lax.axis_index("island")
    shard = lax.axis_index("fsdp")
    core = lax.rem(shard, 2)
    chip = shard // 2
    partner = (island, chip * 2 + 1 - core)

    def peer(step):
        return (island, lax.rem(chip + step, chips) * 2 + core)

    def back(step):
        return (island, lax.rem(chip + chips - step, chips) * 2 + core)

    targets = [partner] + [peer(step) for step in range(1, chips)]
    if chunks:
        groups = islands // 2
        side = lax.rem(island, 2)
        line = island // 2
        across = (line * 2 + 1 - side, shard)

        def along(step):
            return (lax.rem(line + step, groups) * 2 + side, shard)

        targets += [across] + [along(step) for step in range(1, groups)]

    loads = [
        pltpu.make_async_copy(source, place, lsem.at[index])
        for index, (source, place) in enumerate(((w_hbm, w), (x_hbm, x), (cot_hbm, cot)))
    ]
    for load in loads:
        load.start()

    barrier = pltpu.get_barrier_semaphore()
    for target in targets:
        pl.semaphore_signal(barrier, inc=1, device_id=target, device_id_type=MESH)
    pl.semaphore_wait(barrier, len(targets))

    def remote(src, dst, sems, where, target):
        return pltpu.make_async_remote_copy(
            src_ref=src,
            dst_ref=dst,
            send_sem=sems.at[(0,) + where],
            recv_sem=sems.at[(1,) + where],
            device_id=target,
            device_id_type=MESH,
        )

    def columns(start):
        return pl.ds(pl.multiple_of(start, rows), rows)

    copies = []

    def begin(copy):
        copy.start()
        copies.append(copy)
        return copy

    y1 = []
    for step in range(1, chips):
        there = lax.rem(chip + step, chips)
        y1.append(begin(remote(
            x_hbm.at[:, pl.ds(pl.multiple_of(there * 2 * rows, 2 * rows), 2 * rows)],
            xin.at[step - 1], ysem, (step - 1,), peer(step))))
    if chunks:
        half = rows // 2
        size = half // chunks
        unit = size // groups
        p1 = [
            begin(remote(
                w_hbm.at[pl.ds(pl.multiple_of((1 - side) * half + q * size, size), size)],
                p1buf.at[q], s1, (q,), across))
            for q in range(chunks)
        ]
    wcopy = begin(remote(w_hbm, wp, csem, (0,), partner))
    xcopy = [begin(remote(
        x_hbm.at[:, columns((chip * 2 + 1 - core) * rows)], xp.at[0], csem, (1,), partner))]

    p2, p3, p4 = {}, {}, {}

    def pair_sum(q):
        p1[q].wait_recv()
        mine = w[pl.ds(pl.multiple_of(side * half + q * size, size), size), :]
        part[q] = (mine.astype(jnp.float32) + p1buf[q].astype(jnp.float32)).astype(jnp.bfloat16)
        for step in range(1, groups):
            there = lax.rem(line + step, groups)
            p2[q, step] = begin(remote(
                part.at[q, pl.ds(pl.multiple_of(there * unit, unit), unit)],
                p2buf.at[q, step - 1], s2, (q, step - 1), along(step)))

    def line_sum(q):
        total = part[q, pl.ds(pl.multiple_of(line * unit, unit), unit), :].astype(jnp.float32)
        for step in range(1, groups):
            p2[q, step].wait_recv()
            total += p2buf[q, step - 1].astype(jnp.float32)
        place = pl.ds(pl.multiple_of(side * half + q * size + line * unit, unit), unit)
        gathered[place, :] = (total / islands).astype(jnp.bfloat16)
        for step in range(1, groups):
            p3[q, step] = begin(remote(
                gathered.at[place], gathered.at[place], s3, (q, step - 1), along(step)))

    def return_half(q):
        for step in range(1, groups):
            p3[q, step].wait_recv()
        place = pl.ds(pl.multiple_of(side * half + q * size, size), size)
        p4[q] = begin(remote(gathered.at[place], gathered.at[place], s4, (q,), across))

    def product(left, right):
        return jnp.dot(left, right, preferred_element_type=jnp.float32)

    stages = []
    for t in range(chunks + 3 if chunks else 0):
        if t < chunks:
            stages.append((pair_sum, t))
        if 0 <= t - 3 < chunks:
            stages.append((return_half, t - 3))
        if 0 <= t - 1 < chunks:
            stages.append((line_sum, t - 1))

    def advance(last):
        if last in stages:
            for stage, q in stages[: stages.index(last) + 1]:
                stage(q)
            del stages[: stages.index(last) + 1]

    for load in loads:
        load.wait()
    advance((pair_sum, min(1, chunks - 1)))
    wcopy.wait_recv()
    own[...] = product(x[:, columns(shard * rows)], w[...]) + product(
        x[:, columns((chip * 2 + 1 - core) * rows)], wp[...])
    advance((pair_sum, chunks - 1))

    y3 = []
    for step in range(1, chips):
        y1[step - 1].wait_recv()
        xcopy.append(begin(remote(
            xin.at[step - 1, :, columns((1 - core) * rows)], xp.at[step], csem, (step + 1,), partner)))
        psend[step - 1] = (product(xin[step - 1, :, columns(core * rows)], w[...]) + product(
            xin[step - 1, :, columns((1 - core) * rows)], wp[...])).astype(jnp.bfloat16)
        y3.append(begin(remote(
            psend.at[step - 1], precv.at[step - 1], psem, (step - 1,), back(step))))
    advance((line_sum, chunks - 1))

    keys = own[...]
    for step in range(1, chips):
        y3[step - 1].wait_recv()
        keys += precv[step - 1].astype(jnp.float32)
    keys = keys * scale
    for head in range(width // HEAD_DIM):
        lanes = slice(head * HEAD_DIM, (head + 1) * HEAD_DIM)
        kg[:, lanes] = head_backward(keys[:, lanes], cot[:, lanes].astype(jnp.float32), scale)
    y4 = [
        begin(remote(kg, kgin.at[step - 1], ksem, (step - 1,), peer(step)))
        for step in range(1, chips)
    ]
    forwards = [begin(remote(kg, kgp.at[0], fsem, (0,), partner))]

    tile = min(256, rows)

    def add_block(read, upstream, first=False):
        @pl.loop(0, rows // tile)
        def _(t):
            start = pl.multiple_of(t * tile, tile)
            term = lax.dot_general(
                read(start), upstream[...], (((0,), (0,)), ((), ())),
                preferred_element_type=jnp.float32,
            ).astype(jnp.bfloat16).astype(jnp.float32)
            place = pl.ds(start, tile)
            grad[place, :] = term if first else grad[place, :] + term

    def lane(base):
        def at(start):
            return pl.ds(pl.multiple_of(base + start, tile), tile)
        return at

    mine = lane(shard * rows)
    add_block(lambda start: x[:, mine(start)], kg, first=True)
    forwards[0].wait_recv()
    xcopy[0].wait_recv()
    add_block(lambda start: xp[0, :, pl.ds(start, tile)], kgp.at[0])
    advance((return_half, chunks - 2))
    inner = lane(core * rows)
    for step in range(1, chips):
        y4[step - 1].wait_recv()
        forwards.append(begin(remote(
            kgin.at[step - 1], kgp.at[step], fsem, (step,), partner)))
        add_block(lambda start: xin[step - 1, :, inner(start)], kgin.at[step - 1])
    advance((return_half, chunks - 1))
    for step in range(1, chips):
        xcopy[step].wait_recv()
        forwards[step].wait_recv()
        add_block(lambda start: xp[step, :, pl.ds(start, tile)], kgp.at[step])
    if chunks:
        for q in range(chunks):
            p4[q].wait_recv()
        mean[...] = gathered[...]
    for copy in copies:
        copy.wait_send()


def local(
    local_weights, adam_first, adam_second, global_weights, outer_momentum, inputs, key_cotangent
):
    weights = local_weights[0]
    tokens = inputs[0]
    rows, width = weights.shape
    count, depth = tokens.shape
    scale = float(depth) ** (-0.5)
    islands, shards = lax.axis_size("island"), lax.axis_size("fsdp")
    chips = shards // 2
    others = max(chips - 1, 1)
    chunks = chunk_count(rows, islands)
    bf16, f32 = jnp.bfloat16, jnp.float32
    dma = pltpu.SemaphoreType.DMA
    out_shape = [jax.ShapeDtypeStruct((rows, width), f32)]
    scratch = [
        pltpu.VMEM((rows, width), bf16),
        pltpu.VMEM((count, depth), bf16),
        pltpu.VMEM((count, width), bf16),
        dma((3,)),
        pltpu.VMEM((rows, width), bf16),
        pltpu.VMEM((others, count, 2 * rows), bf16),
        pltpu.VMEM((chips, count, rows), bf16),
        pltpu.VMEM((others, count, width), bf16),
        pltpu.VMEM((others, count, width), bf16),
        pltpu.VMEM((others, count, width), bf16),
        pltpu.VMEM((chips, count, width), bf16),
        pltpu.VMEM((count, width), bf16),
        pltpu.VMEM((count, width), f32),
        dma((2, others)),
        dma((2, others)),
        dma((2, others)),
        dma((2, chips + 1)),
        dma((2, chips)),
    ]
    if chunks:
        groups = islands // 2
        size = rows // 2 // chunks
        out_shape.append(jax.ShapeDtypeStruct((rows, width), bf16))
        scratch += [
            pltpu.VMEM((chunks, size, width), bf16),
            pltpu.VMEM((chunks, size, width), bf16),
            pltpu.VMEM((chunks, groups - 1, size // groups, width), bf16),
            pltpu.VMEM((rows, width), bf16),
            dma((2, chunks)),
            dma((2, chunks, groups - 1)),
            dma((2, chunks, groups - 1)),
            dma((2, chunks)),
        ]
    vmem = pl.BlockSpec(memory_space=pltpu.VMEM)
    results = pl.pallas_call(
        functools.partial(exchange, islands, shards, chunks, scale),
        out_shape=out_shape,
        in_specs=[pl.BlockSpec(memory_space=pltpu.HBM)] * 3,
        out_specs=[vmem] * len(out_shape),
        scratch_shapes=scratch,
        compiler_params=pltpu.CompilerParams(
            collective_id=0, has_side_effects=True, vmem_limit_bytes=40 * 1024 * 1024
        ),
    )(*(pltpu.with_memory_space_constraint(a, pltpu.HBM) for a in (weights, tokens, key_cotangent[0])))
    gradient = results[0]
    if chunks:
        mean_local = results[1].astype(jnp.float32)
    else:
        mean_local = lax.psum(weights.astype(jnp.float32), "island") / islands
    outer_grad = global_weights - mean_local
    new_momentum = outer_beta * outer_momentum + outer_grad
    new_global = global_weights - outer_rate * (outer_grad + outer_beta * new_momentum)
    first_new = beta_one * adam_first[0].astype(jnp.float32) + (1.0 - beta_one) * gradient
    second_new = (
        beta_two * adam_second[0].astype(jnp.float32) + (1.0 - beta_two) * gradient * gradient
    )
    current = weights.astype(jnp.float32)
    inner = current - inner_rate * (
        first_new / (jnp.sqrt(second_new) + adam_epsilon) + weight_decay * current
    )
    merged = merge_weight * inner + (1.0 - merge_weight) * new_global
    return (
        merged.astype(jnp.bfloat16)[None],
        first_new.astype(jnp.bfloat16)[None],
        second_new.astype(jnp.bfloat16)[None],
        new_global,
        new_momentum,
    )


def solution(mesh):
    placed = (
        P("island", "fsdp", None),
        P("island", "fsdp", None),
        P("island", "fsdp", None),
        P("fsdp", None),
        P("fsdp", None),
        P("island", "fsdp", None),
        P("island", "fsdp", None),
    )
    return jax.shard_map(
        local,
        mesh=mesh,
        in_specs=placed,
        out_specs=(
            P("island", "fsdp", None),
            P("island", "fsdp", None),
            P("island", "fsdp", None),
            P("fsdp", None),
            P("fsdp", None),
        ),
        check_vma=False,
    )
```

```python
import functools

import jax
import jax.numpy as jnp
from jax import lax
from jax.experimental import pallas as pl
from jax.experimental.pallas import tpu as pltpu
from jax.sharding import PartitionSpec as P

HEAD_DIM = 128
MESH = pl.DeviceIdType.MESH

beta_one = 0.9
beta_two = 0.95
inner_rate = 0.02
weight_decay = 0.1
adam_epsilon = 1e-08
norm_epsilon = 1e-06
outer_rate = 0.7
outer_beta = 0.9
merge_weight = 0.5


def chunk_count(rows, islands):
    for chunks in (8, 4, 2, 1):
        if islands & (islands - 1) == 0 and rows % (islands * chunks * 16) == 0:
            return chunks
    return 0


def head_backward(keys, upstream, scale):
    squares = jnp.mean(keys * keys, axis=-1, keepdims=True)
    inverse = lax.rsqrt(squares + norm_epsilon)
    normed = keys * inverse
    projected = jnp.mean(upstream * normed, axis=-1, keepdims=True)
    return (inverse * (upstream - normed * projected) * scale).astype(jnp.bfloat16)


def exchange(islands, shards, chunks, scale, *refs):
    w_hbm, x_hbm, cot_hbm = refs[:3]
    if chunks:
        (grad, mean, w, x, cot, lsem, wp, xin, xp, psend, precv, kgin, kgp, kg, own,
         ysem, psem, ksem, csem, fsem, landed, part, gathered, hsem) = refs[3:]
    else:
        (grad, w, x, cot, lsem, wp, xin, xp, psend, precv, kgin, kgp, kg, own,
         ysem, psem, ksem, csem, fsem) = refs[3:]
    rows, width = w.shape
    chips = shards // 2
    island = lax.axis_index("island")
    shard = lax.axis_index("fsdp")
    core = lax.rem(shard, 2)
    chip = shard // 2
    partner = (island, chip * 2 + 1 - core)

    def peer(step):
        return (island, lax.rem(chip + step, chips) * 2 + core)

    def back(step):
        return (island, lax.rem(chip + chips - step, chips) * 2 + core)

    targets = [partner] + [peer(step) for step in range(1, chips)]
    if chunks:
        levels = islands.bit_length() - 1
        sides = [lax.rem(island // 2**bit, 2) for bit in range(levels)]
        mates = [(island + (1 - 2 * sides[bit]) * 2**bit, shard) for bit in range(levels)]
        targets += mates

    loads = [
        pltpu.make_async_copy(source, place, lsem.at[index])
        for index, (source, place) in enumerate(((w_hbm, w), (x_hbm, x), (cot_hbm, cot)))
    ]
    for load in loads:
        load.start()

    barrier = pltpu.get_barrier_semaphore()
    for target in targets:
        pl.semaphore_signal(barrier, inc=1, device_id=target, device_id_type=MESH)
    pl.semaphore_wait(barrier, len(targets))

    def remote(src, dst, sems, where, target):
        return pltpu.make_async_remote_copy(
            src_ref=src,
            dst_ref=dst,
            send_sem=sems.at[(0,) + where],
            recv_sem=sems.at[(1,) + where],
            device_id=target,
            device_id_type=MESH,
        )

    def columns(start):
        return pl.ds(pl.multiple_of(start, rows), rows)

    copies = []

    def begin(copy):
        copy.start()
        copies.append(copy)
        return copy

    y1 = []
    for step in range(1, chips):
        there = lax.rem(chip + step, chips)
        y1.append(begin(remote(
            x_hbm.at[:, pl.ds(pl.multiple_of(there * 2 * rows, 2 * rows), 2 * rows)],
            xin.at[step - 1], ysem, (step - 1,), peer(step))))
    halves, returns = {}, {}
    if chunks:
        span = rows // chunks
        orders = [
            [1, 0] + list(range(2, levels)) if levels > 1 and q % 2 == 1 else list(range(levels))
            for q in range(chunks)
        ]
        starts = []
        for q in range(chunks):
            begins = [q * span]
            for level, bit in enumerate(orders[q]):
                begins.append(begins[level] + sides[bit] * (span >> (level + 1)))
            starts.append(begins)

    def segment(q, level):
        return pl.ds(pl.multiple_of(starts[q][level], span >> level), span >> level)

    def landing(level):
        return pl.ds(span - (span >> level), span >> (level + 1))

    def send_half(q, level):
        bit, size = orders[q][level], span >> (level + 1)
        away = starts[q][level] + (1 - sides[bit]) * size
        source = part if level else w_hbm
        halves[q, level] = begin(remote(
            source.at[pl.ds(pl.multiple_of(away, size), size)],
            landed.at[q, landing(level)], hsem, (q, level), mates[bit]))

    def send_back(q, level):
        place = segment(q, level + 1)
        returns[q, level] = begin(remote(
            gathered.at[place], gathered.at[place], hsem, (q, levels + level),
            mates[orders[q][level]]))

    for q in range(chunks):
        send_half(q, 0)
    wcopy = begin(remote(w_hbm, wp, csem, (0,), partner))
    xcopy = [begin(remote(
        x_hbm.at[:, columns((chip * 2 + 1 - core) * rows)], xp.at[0], csem, (1,), partner))]

    def step_of(q, stage):
        if stage < levels:
            halves[q, stage].wait_recv()
            place = segment(q, stage + 1)
            held = (part if stage else w)[place, :].astype(jnp.float32)
            total = held + landed[q, landing(stage), :].astype(jnp.float32)
            if stage + 1 < levels:
                part[place, :] = total.astype(jnp.bfloat16)
                send_half(q, stage + 1)
            else:
                gathered[place, :] = (total / islands).astype(jnp.bfloat16)
                send_back(q, levels - 1)
        else:
            level = 2 * levels - 1 - stage
            returns[q, level].wait_recv()
            if level:
                send_back(q, level - 1)

    def product(left, right):
        return jnp.dot(left, right, preferred_element_type=jnp.float32)

    stages = []
    for q in range(chunks):
        for stage in range(2 * levels):
            late = (q // 2) * 4.0 / chunks
            stages.append((stage + late, q, stage))
    stages.sort()

    def advance(until):
        while stages and stages[0][0] <= until:
            step_of(*stages.pop(0)[1:])

    for load in loads:
        load.wait()
    advance(0.5)
    wcopy.wait_recv()
    own[...] = product(x[:, columns(shard * rows)], w[...]) + product(
        x[:, columns((chip * 2 + 1 - core) * rows)], wp[...])
    advance(3.3)

    y3 = []
    for step in range(1, chips):
        y1[step - 1].wait_recv()
        xcopy.append(begin(remote(
            xin.at[step - 1, :, columns((1 - core) * rows)], xp.at[step], csem, (step + 1,), partner)))
        psend[step - 1] = (product(xin[step - 1, :, columns(core * rows)], w[...]) + product(
            xin[step - 1, :, columns((1 - core) * rows)], wp[...])).astype(jnp.bfloat16)
        y3.append(begin(remote(
            psend.at[step - 1], precv.at[step - 1], psem, (step - 1,), back(step))))
    advance(5.1)

    keys = own[...]
    for step in range(1, chips):
        y3[step - 1].wait_recv()
        keys += precv[step - 1].astype(jnp.float32)
    keys = keys * scale
    for head in range(width // HEAD_DIM):
        lanes = slice(head * HEAD_DIM, (head + 1) * HEAD_DIM)
        kg[:, lanes] = head_backward(keys[:, lanes], cot[:, lanes].astype(jnp.float32), scale)
    y4 = [
        begin(remote(kg, kgin.at[step - 1], ksem, (step - 1,), peer(step)))
        for step in range(1, chips)
    ]
    forwards = [begin(remote(kg, kgp.at[0], fsem, (0,), partner))]

    tile = min(256, rows)

    def add_block(read, upstream, first=False):
        @pl.loop(0, rows // tile)
        def _(t):
            start = pl.multiple_of(t * tile, tile)
            term = lax.dot_general(
                read(start), upstream[...], (((0,), (0,)), ((), ())),
                preferred_element_type=jnp.float32,
            ).astype(jnp.bfloat16).astype(jnp.float32)
            place = pl.ds(start, tile)
            grad[place, :] = term if first else grad[place, :] + term

    def lane(base):
        def at(start):
            return pl.ds(pl.multiple_of(base + start, tile), tile)
        return at

    mine = lane(shard * rows)
    add_block(lambda start: x[:, mine(start)], kg, first=True)
    forwards[0].wait_recv()
    xcopy[0].wait_recv()
    add_block(lambda start: xp[0, :, pl.ds(start, tile)], kgp.at[0])
    advance(6.4)
    inner = lane(core * rows)
    for step in range(1, chips):
        y4[step - 1].wait_recv()
        forwards.append(begin(remote(
            kgin.at[step - 1], kgp.at[step], fsem, (step,), partner)))
        add_block(lambda start: xin[step - 1, :, inner(start)], kgin.at[step - 1])
    advance(6.9)
    for step in range(1, chips):
        xcopy[step].wait_recv()
        forwards[step].wait_recv()
        add_block(lambda start: xp[step, :, pl.ds(start, tile)], kgp.at[step])
    advance(1000)
    if chunks:
        mean[...] = gathered[...]
    for copy in copies:
        copy.wait_send()


def local(
    local_weights, adam_first, adam_second, global_weights, outer_momentum, inputs, key_cotangent
):
    weights = local_weights[0]
    tokens = inputs[0]
    rows, width = weights.shape
    count, depth = tokens.shape
    scale = float(depth) ** (-0.5)
    islands, shards = lax.axis_size("island"), lax.axis_size("fsdp")
    chips = shards // 2
    others = max(chips - 1, 1)
    chunks = chunk_count(rows, islands)
    bf16, f32 = jnp.bfloat16, jnp.float32
    dma = pltpu.SemaphoreType.DMA
    out_shape = [jax.ShapeDtypeStruct((rows, width), f32)]
    scratch = [
        pltpu.VMEM((rows, width), bf16),
        pltpu.VMEM((count, depth), bf16),
        pltpu.VMEM((count, width), bf16),
        dma((3,)),
        pltpu.VMEM((rows, width), bf16),
        pltpu.VMEM((others, count, 2 * rows), bf16),
        pltpu.VMEM((chips, count, rows), bf16),
        pltpu.VMEM((others, count, width), bf16),
        pltpu.VMEM((others, count, width), bf16),
        pltpu.VMEM((others, count, width), bf16),
        pltpu.VMEM((chips, count, width), bf16),
        pltpu.VMEM((count, width), bf16),
        pltpu.VMEM((count, width), f32),
        dma((2, others)),
        dma((2, others)),
        dma((2, others)),
        dma((2, chips + 1)),
        dma((2, chips)),
    ]
    if chunks:
        levels = islands.bit_length() - 1
        out_shape.append(jax.ShapeDtypeStruct((rows, width), bf16))
        scratch += [
            pltpu.VMEM((chunks, rows // chunks, width), bf16),
            pltpu.VMEM((rows, width), bf16),
            pltpu.VMEM((rows, width), bf16),
            dma((2, chunks, 2 * levels)),
        ]
    vmem = pl.BlockSpec(memory_space=pltpu.VMEM)
    results = pl.pallas_call(
        functools.partial(exchange, islands, shards, chunks, scale),
        out_shape=out_shape,
        in_specs=[pl.BlockSpec(memory_space=pltpu.HBM)] * 3,
        out_specs=[vmem] * len(out_shape),
        scratch_shapes=scratch,
        compiler_params=pltpu.CompilerParams(
            collective_id=0, has_side_effects=True, vmem_limit_bytes=40 * 1024 * 1024
        ),
    )(*(pltpu.with_memory_space_constraint(a, pltpu.HBM) for a in (weights, tokens, key_cotangent[0])))
    gradient = results[0]
    if chunks:
        mean_local = results[1].astype(jnp.float32)
    else:
        mean_local = lax.psum(weights.astype(jnp.float32), "island") / islands
    outer_grad = global_weights - mean_local
    new_momentum = outer_beta * outer_momentum + outer_grad
    new_global = global_weights - outer_rate * (outer_grad + outer_beta * new_momentum)
    first_new = beta_one * adam_first[0].astype(jnp.float32) + (1.0 - beta_one) * gradient
    second_new = (
        beta_two * adam_second[0].astype(jnp.float32) + (1.0 - beta_two) * gradient * gradient
    )
    current = weights.astype(jnp.float32)
    inner = current - inner_rate * (
        first_new / (jnp.sqrt(second_new) + adam_epsilon) + weight_decay * current
    )
    merged = merge_weight * inner + (1.0 - merge_weight) * new_global
    return (
        merged.astype(jnp.bfloat16)[None],
        first_new.astype(jnp.bfloat16)[None],
        second_new.astype(jnp.bfloat16)[None],
        new_global,
        new_momentum,
    )


def solution(mesh):
    placed = (
        P("island", "fsdp", None),
        P("island", "fsdp", None),
        P("island", "fsdp", None),
        P("fsdp", None),
        P("fsdp", None),
        P("island", "fsdp", None),
        P("island", "fsdp", None),
    )
    return jax.shard_map(
        local,
        mesh=mesh,
        in_specs=placed,
        out_specs=(
            P("island", "fsdp", None),
            P("island", "fsdp", None),
            P("island", "fsdp", None),
            P("fsdp", None),
            P("fsdp", None),
        ),
        check_vma=False,
    )
```

```python
import functools

import jax
import jax.numpy as jnp
from jax import lax
from jax.experimental import pallas as pl
from jax.experimental.pallas import tpu as pltpu
from jax.sharding import PartitionSpec as P

HEAD_DIM = 128
MESH = pl.DeviceIdType.MESH

beta_one = 0.9
beta_two = 0.95
inner_rate = 0.02
weight_decay = 0.1
adam_epsilon = 1e-08
norm_epsilon = 1e-06
outer_rate = 0.7
outer_beta = 0.9
merge_weight = 0.5


def chunk_count(rows, islands):
    for chunks in (8, 4, 2, 1):
        if islands & (islands - 1) == 0 and rows % (islands * chunks * 16) == 0:
            return chunks
    return 0


def head_backward(keys, upstream, scale):
    squares = jnp.mean(keys * keys, axis=-1, keepdims=True)
    inverse = lax.rsqrt(squares + norm_epsilon)
    normed = keys * inverse
    projected = jnp.mean(upstream * normed, axis=-1, keepdims=True)
    return (inverse * (upstream - normed * projected) * scale).astype(jnp.bfloat16)


def exchange(islands, shards, chunks, scale, *refs):
    w_hbm, x_hbm, cot_hbm = refs[:3]
    if chunks:
        (grad, mean, w, x, cot, lsem, wp, xin, xp, psend, precv, kgin, kgp, kg, own,
         ysem, psem, ksem, csem, fsem, landed, part, gathered, hsem) = refs[3:]
    else:
        (grad, w, x, cot, lsem, wp, xin, xp, psend, precv, kgin, kgp, kg, own,
         ysem, psem, ksem, csem, fsem) = refs[3:]
    rows, width = w.shape
    chips = shards // 2
    island = lax.axis_index("island")
    shard = lax.axis_index("fsdp")
    core = lax.rem(shard, 2)
    chip = shard // 2
    partner = (island, chip * 2 + 1 - core)

    def peer(step):
        return (island, lax.rem(chip + step, chips) * 2 + core)

    def back(step):
        return (island, lax.rem(chip + chips - step, chips) * 2 + core)

    targets = [partner] + [peer(step) for step in range(1, chips)]
    if chunks:
        levels = islands.bit_length() - 1
        sides = [lax.rem(island // 2**bit, 2) for bit in range(levels)]
        mates = [(island + (1 - 2 * sides[bit]) * 2**bit, shard) for bit in range(levels)]
        targets += mates

    loads = [
        pltpu.make_async_copy(source, place, lsem.at[index])
        for index, (source, place) in enumerate(((w_hbm, w), (x_hbm, x), (cot_hbm, cot)))
    ]
    for load in loads:
        load.start()

    barrier = pltpu.get_barrier_semaphore()
    for target in targets:
        pl.semaphore_signal(barrier, inc=1, device_id=target, device_id_type=MESH)
    pl.semaphore_wait(barrier, len(targets))

    def remote(src, dst, sems, where, target):
        return pltpu.make_async_remote_copy(
            src_ref=src,
            dst_ref=dst,
            send_sem=sems.at[(0,) + where],
            recv_sem=sems.at[(1,) + where],
            device_id=target,
            device_id_type=MESH,
        )

    def columns(start):
        return pl.ds(pl.multiple_of(start, rows), rows)

    copies = []

    def begin(copy):
        copy.start()
        copies.append(copy)
        return copy

    y1 = []
    for step in range(1, chips):
        there = lax.rem(chip + step, chips)
        y1.append(begin(remote(
            x_hbm.at[:, pl.ds(pl.multiple_of(there * 2 * rows, 2 * rows), 2 * rows)],
            xin.at[step - 1], ysem, (step - 1,), peer(step))))
    halves, returns = {}, {}
    if chunks:
        span = rows // chunks
        orders = [
            [1, 0] + list(range(2, levels)) if levels > 1 and q % 2 == 1 else list(range(levels))
            for q in range(chunks)
        ]
        starts = []
        for q in range(chunks):
            begins = [q * span]
            for level, bit in enumerate(orders[q]):
                begins.append(begins[level] + sides[bit] * (span >> (level + 1)))
            starts.append(begins)

    def segment(q, level):
        return pl.ds(pl.multiple_of(starts[q][level], span >> level), span >> level)

    def landing(level):
        return pl.ds(span - (span >> level), span >> (level + 1))

    def send_half(q, level):
        bit, size = orders[q][level], span >> (level + 1)
        away = starts[q][level] + (1 - sides[bit]) * size
        source = part if level else w_hbm
        halves[q, level] = begin(remote(
            source.at[pl.ds(pl.multiple_of(away, size), size)],
            landed.at[q, landing(level)], hsem, (q, level), mates[bit]))

    def send_back(q, level):
        place = segment(q, level + 1)
        returns[q, level] = begin(remote(
            gathered.at[place], gathered.at[place], hsem, (q, levels + level),
            mates[orders[q][level]]))

    for q in range(chunks):
        send_half(q, 0)
    wcopy = begin(remote(w_hbm, wp, csem, (0,), partner))
    xcopy = [begin(remote(
        x_hbm.at[:, columns((chip * 2 + 1 - core) * rows)], xp.at[0], csem, (1,), partner))]

    def step_of(q, stage):
        if stage < levels:
            halves[q, stage].wait_recv()
            place = segment(q, stage + 1)
            held = (part if stage else w)[place, :].astype(jnp.float32)
            total = held + landed[q, landing(stage), :].astype(jnp.float32)
            if stage + 1 < levels:
                part[place, :] = total.astype(jnp.bfloat16)
                send_half(q, stage + 1)
            else:
                gathered[place, :] = (total / islands).astype(jnp.bfloat16)
                send_back(q, levels - 1)
        else:
            level = 2 * levels - 1 - stage
            returns[q, level].wait_recv()
            if level:
                send_back(q, level - 1)

    def product(left, right):
        return jnp.dot(left, right, preferred_element_type=jnp.float32)

    stages = []
    for q in range(chunks):
        for stage in range(2 * levels):
            late = (q // 2) * 6.0 / chunks
            stages.append((stage + late, q, stage))
    stages.sort()

    def advance(until):
        while stages and stages[0][0] <= until:
            step_of(*stages.pop(0)[1:])

    for load in loads:
        load.wait()
    advance(0.5)
    wcopy.wait_recv()
    own[...] = product(x[:, columns(shard * rows)], w[...]) + product(
        x[:, columns((chip * 2 + 1 - core) * rows)], wp[...])
    advance(3.3)

    y3 = []
    for step in range(1, chips):
        y1[step - 1].wait_recv()
        xcopy.append(begin(remote(
            xin.at[step - 1, :, columns((1 - core) * rows)], xp.at[step], csem, (step + 1,), partner)))
        psend[step - 1] = (product(xin[step - 1, :, columns(core * rows)], w[...]) + product(
            xin[step - 1, :, columns((1 - core) * rows)], wp[...])).astype(jnp.bfloat16)
        y3.append(begin(remote(
            psend.at[step - 1], precv.at[step - 1], psem, (step - 1,), back(step))))
    advance(5.1)

    keys = own[...]
    for step in range(1, chips):
        y3[step - 1].wait_recv()
        keys += precv[step - 1].astype(jnp.float32)
    keys = keys * scale
    for head in range(width // HEAD_DIM):
        lanes = slice(head * HEAD_DIM, (head + 1) * HEAD_DIM)
        kg[:, lanes] = head_backward(keys[:, lanes], cot[:, lanes].astype(jnp.float32), scale)
    y4 = [
        begin(remote(kg, kgin.at[step - 1], ksem, (step - 1,), peer(step)))
        for step in range(1, chips)
    ]
    forwards = [begin(remote(kg, kgp.at[0], fsem, (0,), partner))]

    tile = min(256, rows)

    def add_block(read, upstream, first=False):
        @pl.loop(0, rows // tile)
        def _(t):
            start = pl.multiple_of(t * tile, tile)
            term = lax.dot_general(
                read(start), upstream[...], (((0,), (0,)), ((), ())),
                preferred_element_type=jnp.float32,
            ).astype(jnp.bfloat16).astype(jnp.float32)
            place = pl.ds(start, tile)
            grad[place, :] = term if first else grad[place, :] + term

    def lane(base):
        def at(start):
            return pl.ds(pl.multiple_of(base + start, tile), tile)
        return at

    mine = lane(shard * rows)
    add_block(lambda start: x[:, mine(start)], kg, first=True)
    forwards[0].wait_recv()
    xcopy[0].wait_recv()
    add_block(lambda start: xp[0, :, pl.ds(start, tile)], kgp.at[0])
    advance(6.4)
    inner = lane(core * rows)
    for step in range(1, chips):
        y4[step - 1].wait_recv()
        forwards.append(begin(remote(
            kgin.at[step - 1], kgp.at[step], fsem, (step,), partner)))
        add_block(lambda start: xin[step - 1, :, inner(start)], kgin.at[step - 1])
    advance(6.9)
    for step in range(1, chips):
        xcopy[step].wait_recv()
        forwards[step].wait_recv()
        add_block(lambda start: xp[step, :, pl.ds(start, tile)], kgp.at[step])
    advance(1000)
    if chunks:
        mean[...] = gathered[...]
    for copy in copies:
        copy.wait_send()


def local(
    local_weights, adam_first, adam_second, global_weights, outer_momentum, inputs, key_cotangent
):
    weights = local_weights[0]
    tokens = inputs[0]
    rows, width = weights.shape
    count, depth = tokens.shape
    scale = float(depth) ** (-0.5)
    islands, shards = lax.axis_size("island"), lax.axis_size("fsdp")
    chips = shards // 2
    others = max(chips - 1, 1)
    chunks = chunk_count(rows, islands)
    bf16, f32 = jnp.bfloat16, jnp.float32
    dma = pltpu.SemaphoreType.DMA
    out_shape = [jax.ShapeDtypeStruct((rows, width), f32)]
    scratch = [
        pltpu.VMEM((rows, width), bf16),
        pltpu.VMEM((count, depth), bf16),
        pltpu.VMEM((count, width), bf16),
        dma((3,)),
        pltpu.VMEM((rows, width), bf16),
        pltpu.VMEM((others, count, 2 * rows), bf16),
        pltpu.VMEM((chips, count, rows), bf16),
        pltpu.VMEM((others, count, width), bf16),
        pltpu.VMEM((others, count, width), bf16),
        pltpu.VMEM((others, count, width), bf16),
        pltpu.VMEM((chips, count, width), bf16),
        pltpu.VMEM((count, width), bf16),
        pltpu.VMEM((count, width), f32),
        dma((2, others)),
        dma((2, others)),
        dma((2, others)),
        dma((2, chips + 1)),
        dma((2, chips)),
    ]
    if chunks:
        levels = islands.bit_length() - 1
        out_shape.append(jax.ShapeDtypeStruct((rows, width), bf16))
        scratch += [
            pltpu.VMEM((chunks, rows // chunks, width), bf16),
            pltpu.VMEM((rows, width), bf16),
            pltpu.VMEM((rows, width), bf16),
            dma((2, chunks, 2 * levels)),
        ]
    vmem = pl.BlockSpec(memory_space=pltpu.VMEM)
    results = pl.pallas_call(
        functools.partial(exchange, islands, shards, chunks, scale),
        out_shape=out_shape,
        in_specs=[pl.BlockSpec(memory_space=pltpu.HBM)] * 3,
        out_specs=[vmem] * len(out_shape),
        scratch_shapes=scratch,
        compiler_params=pltpu.CompilerParams(
            collective_id=0, has_side_effects=True, vmem_limit_bytes=40 * 1024 * 1024
        ),
    )(*(pltpu.with_memory_space_constraint(a, pltpu.HBM) for a in (weights, tokens, key_cotangent[0])))
    gradient = results[0]
    if chunks:
        mean_local = results[1].astype(jnp.float32)
    else:
        mean_local = lax.psum(weights.astype(jnp.float32), "island") / islands
    outer_grad = global_weights - mean_local
    new_momentum = outer_beta * outer_momentum + outer_grad
    new_global = global_weights - outer_rate * (outer_grad + outer_beta * new_momentum)
    first_new = beta_one * adam_first[0].astype(jnp.float32) + (1.0 - beta_one) * gradient
    second_new = (
        beta_two * adam_second[0].astype(jnp.float32) + (1.0 - beta_two) * gradient * gradient
    )
    current = weights.astype(jnp.float32)
    inner = current - inner_rate * (
        first_new / (jnp.sqrt(second_new) + adam_epsilon) + weight_decay * current
    )
    merged = merge_weight * inner + (1.0 - merge_weight) * new_global
    return (
        merged.astype(jnp.bfloat16)[None],
        first_new.astype(jnp.bfloat16)[None],
        second_new.astype(jnp.bfloat16)[None],
        new_global,
        new_momentum,
    )


def solution(mesh):
    placed = (
        P("island", "fsdp", None),
        P("island", "fsdp", None),
        P("island", "fsdp", None),
        P("fsdp", None),
        P("fsdp", None),
        P("island", "fsdp", None),
        P("island", "fsdp", None),
    )
    return jax.shard_map(
        local,
        mesh=mesh,
        in_specs=placed,
        out_specs=(
            P("island", "fsdp", None),
            P("island", "fsdp", None),
            P("island", "fsdp", None),
            P("fsdp", None),
            P("fsdp", None),
        ),
        check_vma=False,
    )
```
